32 devices in a mesh: leaf: 8 (over z, y), tile: 4 (over x, core).
Axes of the slice: x: 2, y: 2, z: 4, core: 2. Of those that a mesh axis runs over, the one named last changes fastest.
Arguments:
- rhs_leaf: float32 [16384, 128], P(('leaf', 'tile')), may hold values from -6 to 6
- rhs_sep: float32 [12288, 128], P(('leaf', 'tile')), may hold values from -6 to 6
- leaf_inv: float32 [16384, 2048], P(('leaf', 'tile')), as said below
- leaf_up: float32 [8, 1536, 2048], P('leaf', None, 'tile'), may hold values from -0.0625 to 0.0625
- sep_inv: float32 [12288, 1536], P(('leaf', 'tile')), as said below
- sep_up: float32 [8, 1536, 1536], P('leaf', None, 'tile'), may hold values from -0.078125 to 0.078125
- live_tiles: int32 [8], replicated, may hold values from 6 to 12, as said below
Outputs:
- leaf_result: float32 [16384, 128], P(('leaf', 'tile'))
- sep_result: float32 [12288, 128], P(('leaf', 'tile'))
The draws below stay inside these ranges and needn't reach their ends.
Inputs may be any that keep to these rules, and one draw needn't show every extreme that they name: `leaf_inv`: each block of 2048 rows is lower triangular. `sep_inv`: each block of 1536 rows is lower triangular. `live_tiles`: some separator of the lowest level has all 12 tiles live.
All inputs are finite; a program needn't handle non-finite values.
Results may differ from the reference program's by a relative error of at most 0.0003.
Values sent between devices are 32-bit elements; how exact they have to be, the bound alone decides.
A program may use at most 128 MiB of HBM per device.

```python
import math
import jax
import jax.numpy as jnp
import numpy as np
from jax import lax

COLS = 128
TILE = 128
SEP_TILES = 12
SEP_ROWS = 1536
LEAF_ROWS = 2048
LEVELS = 3
FIRST = 3
N_LEAF = 8


def triangle(key, blocks, order):
    first, second = jax.random.split(key)
    total_rows = blocks * order
    within = jnp.arange(total_rows, dtype=jnp.int32)[:, None] % order
    columns = jnp.arange(order, dtype=jnp.int32)[None, :]
    spread = jax.random.normal(first, (total_rows, order), jnp.float32)
    diagonal = jax.random.uniform(second, (total_rows, 1), jnp.float32, 0.7, 1.4)
    lower = jnp.where(columns < within, spread * (0.6 / math.sqrt(order)), 0.0)
    return lower + jnp.where(columns == within, diagonal, 0.0)


def draw_leaf_inv(key, part):
    return triangle(jax.random.fold_in(key, 11), N_LEAF, LEAF_ROWS)


def draw_sep_inv(key, part):
    return triangle(jax.random.fold_in(key, 23), N_LEAF, SEP_ROWS)


def draw_live_tiles(key, part):
    first, second = jax.random.split(jax.random.fold_in(key, 37))
    counts = jax.random.randint(first, (N_LEAF,), SEP_TILES // 2, SEP_TILES + 1)
    chosen = jax.random.randint(second, (), 0, N_LEAF // 2)
    places = jnp.arange(N_LEAF, dtype=jnp.int32)
    target = (2 * chosen + FIRST) % N_LEAF
    return jnp.where(places == target, SEP_TILES, counts).astype(jnp.int32)


def level_of(own_key, shape, cuts, low, high):
    factor_of, own = 1.0, jax.random.fold_in(own_key, 6)
    for position, blocks in cuts:
        draws = jnp.exp(jax.random.uniform(jax.random.fold_in(own, position), (blocks,), jnp.float32, low / len(cuts), high / len(cuts)))
        factor_of = factor_of * jnp.repeat(draws, shape[position] // blocks).reshape([-1 if axis == position else 1 for axis in range(len(shape))])
    return factor_of


def normal_values(own_key, shape, width, reach, pieces=(), kind=jnp.bfloat16):
    entries = width * jax.random.normal(own_key, shape, jnp.float32)
    if pieces:
        entries = entries * level_of(own_key, shape, pieces, -0.22, 0.18)
    return jnp.clip(entries, -reach, reach).astype(kind)


def setup_inputs(seed: int = 0) -> dict:
    arg_keys = jax.random.split(jax.random.key(seed), 8)
    rhs_leaf = normal_values(arg_keys[0], (N_LEAF * LEAF_ROWS, COLS), 1.0, 6.0, ((0, 32),), jnp.float32)
    rhs_sep = normal_values(arg_keys[1], (N_LEAF * SEP_ROWS, COLS), 1.0, 6.0, ((0, 32),), jnp.float32)
    leaf_inv = draw_leaf_inv(jax.random.fold_in(arg_keys[7], 71), 0)
    leaf_up = normal_values(arg_keys[3], (N_LEAF, SEP_ROWS, LEAF_ROWS), (4 * LEAF_ROWS) ** -0.5, 0.0625, ((0, 8), (2, 4)), jnp.float32)
    sep_inv = draw_sep_inv(jax.random.fold_in(arg_keys[7], 71), 0)
    sep_up = normal_values(arg_keys[5], (N_LEAF, SEP_ROWS, SEP_ROWS), (4 * SEP_ROWS) ** -0.5, 0.078125, ((0, 8), (2, 4)), jnp.float32)
    live_tiles = draw_live_tiles(jax.random.fold_in(arg_keys[7], 71), 0)
    return {"rhs_leaf": rhs_leaf, "rhs_sep": rhs_sep, "leaf_inv": leaf_inv, "leaf_up": leaf_up, "sep_inv": sep_inv, "sep_up": sep_up, "live_tiles": live_tiles}


HIGHEST = lax.Precision.HIGHEST


def live_rows(live_tiles):
    index = jnp.arange(SEP_ROWS, dtype=jnp.int32)
    return (index[None, :] < live_tiles[:, None] * TILE).astype(jnp.float32)[:, :, None]


def node_numbers(level):
    return np.arange(N_LEAF >> level) * (1 << level) + (1 << (level - 1)) - 1


def to_tree(blocks):
    return jnp.roll(blocks, -FIRST, axis=0)


def from_tree(blocks):
    return jnp.roll(blocks, FIRST, axis=0)


def reference(rhs_leaf, rhs_sep, leaf_inv, leaf_up, sep_inv, sep_up, live_tiles):
    leaf_inverse = to_tree(leaf_inv.reshape(N_LEAF, LEAF_ROWS, LEAF_ROWS))
    sep_inverse = to_tree(sep_inv.reshape(N_LEAF, SEP_ROWS, SEP_ROWS))
    leaf_right = to_tree(rhs_leaf.reshape(N_LEAF, LEAF_ROWS, COLS))
    sep_right = to_tree(rhs_sep.reshape(N_LEAF, SEP_ROWS, COLS))
    leaf_upper = to_tree(leaf_up)
    sep_upper = to_tree(sep_up)
    masks = live_rows(to_tree(live_tiles))
    leaf_solved = jnp.einsum("nab,nbr->nar", leaf_inverse, leaf_right, precision=HIGHEST)
    upward = jnp.einsum("nsc,ncr->nsr", leaf_upper, leaf_solved, precision=HIGHEST)
    sep_solved = jnp.zeros((N_LEAF, SEP_ROWS, COLS), jnp.float32)
    for level in range(1, LEVELS + 1):
        nodes = node_numbers(level)
        if level == 1:
            left_kids, right_kids = nodes, nodes + 1
        else:
            offset = 1 << (level - 2)
            left_kids, right_kids = nodes - offset, nodes + offset
        residue = (sep_right[nodes] - upward[left_kids] - upward[right_kids]) * masks[nodes]
        solved = jnp.einsum("nab,nbr->nar", sep_inverse[nodes], residue, precision=HIGHEST) * masks[nodes]
        sep_solved = sep_solved.at[nodes].set(solved)
        if level < LEVELS:
            upward = upward.at[nodes].set(jnp.einsum("nsc,ncr->nsr", sep_upper[nodes], solved, precision=HIGHEST))
    sep_result = jnp.zeros((N_LEAF, SEP_ROWS, COLS), jnp.float32)
    for level in range(LEVELS, 0, -1):
        nodes = node_numbers(level)
        if level == LEVELS:
            residue = sep_solved[nodes]
        else:
            half = 1 << (level - 1)
            order = np.arange(N_LEAF >> level)
            parents = np.where(order % 2 == 0, nodes + half, nodes - half)
            carried = jnp.einsum("nsc,nsr->ncr", sep_upper[nodes], sep_result[parents], precision=HIGHEST)
            residue = sep_solved[nodes] - carried
        residue = residue * masks[nodes]
        result = jnp.einsum("nab,nar->nbr", sep_inverse[nodes], residue, precision=HIGHEST) * masks[nodes]
        sep_result = sep_result.at[nodes].set(result)
    leaves = np.arange(N_LEAF)
    parents = leaves - leaves % 2
    carried = jnp.einsum("nsc,nsr->ncr", leaf_upper, sep_result[parents], precision=HIGHEST)
    leaf_result = jnp.einsum("nab,nar->nbr", leaf_inverse, leaf_solved - carried, precision=HIGHEST)
    leaf_result = from_tree(leaf_result)
    sep_result = from_tree(sep_result)
    return leaf_result.reshape(N_LEAF * LEAF_ROWS, COLS), sep_result.reshape(N_LEAF * SEP_ROWS, COLS)
```

```python
import functools
import jax
import jax.numpy as jnp
from jax import lax
from jax.experimental import pallas as pl
from jax.experimental.pallas import tpu as pltpu
from jax.sharding import PartitionSpec as P

TILE = 128
PIECES = 2
MESH = pl.DeviceIdType.MESH
F32 = jnp.float32
BF16 = jnp.bfloat16

LEAF_GATHER, LEAF_SUM, SEP_GATHER, SEP_SUM = 0, 3, 6, 9
BACK_GATHER, BACK_SUM, LAST_GATHER, LAST_SUM = 12, 15, 18, 21
KID, ABOVE, LEAF_ABOVE, ABOVE_RIGHT = 24, 26, 27, 28
KINDS = 29


def split(value):
    high = value.astype(BF16)
    return high, (value - high.astype(F32)).astype(BF16)


def times(value, high_ref, low_ref, index, transposed):
    dims = (((1,), (1 if transposed else 0,)), ((), ()))
    rows = value.shape[0]
    high, low = split(value)
    both = jnp.concatenate([high, low], axis=0)
    first = lax.dot_general(both, high_ref[index], dims, preferred_element_type=F32)
    second = lax.dot_general(high, low_ref[index], dims, preferred_element_type=F32)
    return first[:rows] + first[rows:] + second


def kernel(
    leaves,
    live_ref,
    rhs_leaf,
    rhs_sep,
    leaf_inv,
    leaf_up,
    sep_inv,
    sep_up,
    leaf_out,
    sep_out,
    rhs_l,
    rhs_s,
    li,
    lu,
    si,
    su,
    li_h,
    li_l,
    lu_h,
    lu_l,
    si_h,
    si_l,
    su_h,
    su_l,
    gather_l,
    gather_s,
    gather_b,
    gather_c,
    part_l,
    part_s,
    part_b,
    part_c,
    one_l,
    one_s,
    one_b,
    one_c,
    two_l,
    two_s,
    two_b,
    two_c,
    kid,
    solved_l,
    solved_s,
    acc_s,
    acc_l,
    load_sem,
    send_sem,
    recv_sem,
):
    depth = leaves.bit_length() - 1
    first_block = leaves // 4 + 1
    leaf = lax.axis_index("leaf")
    t = lax.axis_index("tile")
    core = t % 2
    half = t // 2
    sib = t + 1 - 2 * core
    acr = (t + 2) % 4
    far = (sib + 2) % 4
    pos = (leaf + leaves - first_block) % leaves
    ahead = pos + 1
    share = rhs_s.shape[0]
    cols = rhs_s.shape[1]
    rows = cols // PIECES

    def block_of(place):
        return (place + leaves + first_block) % leaves

    level_one = ahead % 2 == 1
    has_sep = pos < leaves - 1
    is_top = ahead == leaves // 2
    not_top = jnp.logical_and(has_sep, ahead != leaves // 2)
    has_kids = jnp.logical_and(has_sep, ahead % 2 == 0)
    parent = pos * 0
    side = pos * 0
    reach = pos * 0
    for level in range(1, depth + 1):
        own = (ahead % (1 << level) == (1 << (level - 1))).astype(jnp.int32)
        odd = (ahead // (1 << level)) % 2
        step = 1 << (level - 1)
        parent = parent + own * (pos + step - 2 * step * odd)
        side = side + own * odd
        reach = reach + own * (step // 2)
    up_block = block_of(parent)
    left_block = block_of(pos - reach)
    right_block = block_of(pos + reach)
    pair_block = block_of(pos + 1 - 2 * (pos % 2))

    def loads(kind, source, target, by_column):
        out = []
        for q in range(4):
            if by_column:
                width = target.shape[2]
                view = source.at[:, pl.ds(q * width, width)]
            else:
                height = target.shape[1]
                view = source.at[pl.ds(q * height, height), :]
            out.append(pltpu.make_async_copy(view, target.at[q], load_sem.at[kind, q]))
        return out

    load_rl = pltpu.make_async_copy(rhs_leaf, rhs_l, load_sem.at[4, 0])
    load_rs = pltpu.make_async_copy(rhs_sep, rhs_s, load_sem.at[4, 1])
    load_li = loads(0, leaf_inv, li, True)
    load_lu = loads(1, leaf_up, lu, False)
    load_si = loads(2, sep_inv, si, True)
    load_su = loads(3, sep_up, su, False)
    load_rl.start()
    for copy in load_li + load_lu:
        copy.start()
    load_rs.start()
    for copy in load_si + load_su:
        copy.start()

    barrier = pltpu.get_barrier_semaphore()

    def greet(block, tile):
        pl.semaphore_signal(barrier, inc=1, device_id=(block, tile), device_id_type=MESH)

    greet(leaf, sib)
    greet(leaf, acr)
    greet(pair_block, t)

    @pl.when(not_top)
    def _():
        greet(up_block, t)

    @pl.when(has_kids)
    def _():
        greet(left_block, t)
        greet(right_block, t)

    def split_weights(copies, source, high, low):
        for q in range(4):
            copies[q].wait()
            height = source.shape[1]

            def body(i, carry, q=q):
                at = pl.ds(pl.multiple_of(i * 64, 64), 64)
                h, l = split(source[q, at, :])
                high[q, at, :] = h
                low[q, at, :] = l
                return carry

            lax.fori_loop(0, height // 64, body, 0)

    load_rl.wait()
    gather_l[t] = rhs_l[...].T

    pl.semaphore_wait(
        barrier, 3 + not_top.astype(jnp.int32) + 2 * has_kids.astype(jnp.int32)
    )

    pending = []

    def when(cond, run):
        if cond is None:
            run()
        else:
            pl.when(cond)(run)

    def piece(ref, q, p):
        at = pl.ds(p * rows, rows)
        return lambda: ref.at[at] if q is None else ref.at[q, at]

    def remote(kind, p, source, target, block, tile):
        return pltpu.make_async_remote_copy(
            src_ref=source(),
            dst_ref=target(),
            send_sem=send_sem.at[kind, p],
            recv_sem=recv_sem.at[kind, p],
            device_id=(block, tile),
            device_id_type=MESH,
        )

    def send(kind, p, source, target, block, tile, cond, outer, slot=None):
        def make():
            copy = pltpu.make_async_remote_copy(
                src_ref=source(),
                dst_ref=target(),
                send_sem=send_sem.at[kind, p],
                recv_sem=recv_sem.at[kind if slot is None else slot, p],
                device_id=(block, tile),
                device_id_type=MESH,
            )
            return copy

        when(cond, lambda: make().start())
        pending.append((outer, cond, lambda: make().wait_send()))

    def arrive(kind, p, target):
        remote(kind, p, target, target, leaf, sib).wait_recv()

    def at(p):
        return pl.ds(p * rows, rows)

    low_core, high_core = core == 0, core == 1
    low_half, high_half = half == 0, half == 1

    def gather_send(kind, ref, p, triangle, outer):
        mine = piece(ref, t, p)
        send(kind + 1, p, mine, mine, leaf, acr, low_half if triangle else None, outer)
        send(kind, p, mine, mine, leaf, sib, low_core if triangle else None, outer)

    def gather_use(kind, ref, acc, high, low, triangle, outer, transposed, between=None):
        def add(q, p):
            acc[at(p), :] += times(ref[q, at(p), :], high, low, q, transposed)

        for p in range(PIECES):
            acc[at(p), :] = times(ref[t, at(p), :], high, low, t, transposed)
        if between is not None:
            between()
        for p in range(PIECES):

            def from_sib(p=p):
                arrive(kind, p, piece(ref, sib, p))
                add(sib, p)

            when(high_core if triangle else None, from_sib)
        for p in range(PIECES):

            def from_acr(p=p):
                got = piece(ref, acr, p)
                arrive(kind + 1, p, got)
                remote(kind + 2, p, got, got, leaf, sib).start()
                add(acr, p)

            when(high_half if triangle else None, from_acr)

            def sent(p=p):
                got = piece(ref, acr, p)
                remote(kind + 2, p, got, got, leaf, sib).wait_send()

            pending.append((outer, high_half if triangle else None, sent))
        for p in range(PIECES):

            def from_far(p=p):
                arrive(kind + 2, p, piece(ref, far, p))
                add(far, p)

            when(high_half if triangle else None, from_far)

    def sum_scatter(kind, value, part, one, two, high, low, triangle, outer, transposed, then, between=None):
        over = high_half if triangle else None

        def work(q, p):
            part[q, at(p), :] = times(value[at(p), :], high, low, q, transposed)

        for p in range(PIECES):
            when(over, lambda p=p: work(far, p))
            send(kind, p, piece(part, far, p), piece(one, 0, p), leaf, sib, over, outer)
        for p in range(PIECES):
            when(over, lambda p=p: work(acr, p))
        for p in range(PIECES):

            def pass_on(p=p):
                arrive(kind, p, piece(one, 0, p))
                part[acr, at(p), :] += one[0, at(p), :]

            when(over, pass_on)
            send(kind + 1, p, piece(part, acr, p), piece(two, None, p), leaf, acr, over, outer)
        for p in range(PIECES):
            when(high_core if triangle else None, lambda p=p: work(sib, p))
            send(
                kind + 2,
                p,
                piece(part, sib, p),
                piece(one, 1, p),
                leaf,
                sib,
                high_core if triangle else None,
                outer,
            )
        for p in range(PIECES):
            work(t, p)
        if between is not None:
            between()
        for p in range(PIECES):

            def from_sib(p=p):
                arrive(kind + 2, p, piece(one, 1, p))
                part[t, at(p), :] += one[1, at(p), :]

            when(low_core if triangle else None, from_sib)
        for p in range(PIECES):

            def from_acr(p=p):
                arrive(kind + 1, p, piece(two, None, p))
                part[t, at(p), :] += two[at(p), :]

            when(low_half if triangle else None, from_acr)
            then(p)

    for p in range(PIECES):
        gather_send(LEAF_GATHER, gather_l, p, True, None)
    split_weights(load_li, li, li_h, li_l)
    gather_use(
        LEAF_GATHER,
        gather_l,
        solved_l,
        li_h,
        li_l,
        True,
        None,
        True,
        lambda: split_weights(load_lu, lu, lu_h, lu_l),
    )
    is_odd = pos % 2 == 1
    is_even = pos % 2 == 0

    def leaf_done(p):
        @pl.when(is_even)
        def _():
            kid[0, at(p), :] = part_l[t, at(p), :]

        send(KID, p, piece(part_l, t, p), piece(kid, 1, p), pair_block, t, is_odd, None, KID + 1)

    def prepare():
        split_weights(load_si, si, si_h, si_l)
        split_weights(load_su, su, su_h, su_l)
        load_rs.wait()

    sum_scatter(
        LEAF_SUM, solved_l, part_l, one_l, two_l, lu_h, lu_l, False, None, True, leaf_done, prepare
    )

    live = live_ref[leaf]
    index = lax.broadcasted_iota(jnp.int32, (1, share), 1) + t * share
    mask = jnp.where(index < live * TILE, 1.0, 0.0).astype(F32)

    @pl.when(has_sep)
    def _():
        acc_s[...] = rhs_s[...].T
        for p in range(PIECES):

            @pl.when(has_kids)
            def _():
                arrive(KID, p, piece(kid, 0, p))

            arrive(KID + 1, p, piece(kid, 1, p))
            gather_s[t, at(p), :] = (
                acc_s[at(p), :] - kid[0, at(p), :] - kid[1, at(p), :]
            ) * mask
            gather_send(SEP_GATHER, gather_s, p, True, has_sep)
        gather_use(SEP_GATHER, gather_s, solved_s, si_h, si_l, True, has_sep, True)
        solved_s[...] = solved_s[...] * mask

        @pl.when(not_top)
        def _():
            def sep_done(p):
                def make(wait):
                    copy = pltpu.make_async_remote_copy(
                        src_ref=piece(part_s, t, p)(),
                        dst_ref=kid.at[side, at(p)],
                        send_sem=send_sem.at[ABOVE_RIGHT, p],
                        recv_sem=recv_sem.at[KID + side, p],
                        device_id=(up_block, t),
                        device_id_type=MESH,
                    )
                    return copy.wait_send() if wait else copy.start()

                make(False)
                pending.append((not_top, None, lambda p=p: make(True)))

            sum_scatter(
                SEP_SUM, solved_s, part_s, one_s, two_s, su_h, su_l, False, not_top, True, sep_done
            )
            for p in range(PIECES):
                arrive(ABOVE, p, piece(gather_b, t, p))
                gather_send(BACK_GATHER, gather_b, p, False, not_top)
            gather_use(BACK_GATHER, gather_b, acc_s, su_h, su_l, False, not_top, False)
            solved_s[...] = (solved_s[...] - acc_s[...]) * mask

        def back_done(p):
            part_b[t, at(p), :] = part_b[t, at(p), :] * mask
            mine = piece(part_b, t, p)
            there = piece(gather_b, t, p)
            send(ABOVE, p, mine, there, left_block, t, has_kids, has_sep)
            send(ABOVE_RIGHT + 1, p, mine, there, right_block, t, has_kids, has_sep, ABOVE)

            @pl.when(level_one)
            def _():
                gather_c[t, at(p), :] = part_b[t, at(p), :]

            here = piece(gather_c, t, p)
            send(LEAF_ABOVE, p, here, here, pair_block, t, level_one, has_sep)

        sum_scatter(
            BACK_SUM, solved_s, part_b, one_b, two_b, si_h, si_l, True, has_sep, False, back_done
        )

    for p in range(PIECES):

        @pl.when(is_odd)
        def _():
            arrive(LEAF_ABOVE, p, piece(gather_c, t, p))

        gather_send(LAST_GATHER, gather_c, p, False, None)

    @pl.when(has_sep)
    def _():
        sep_out[...] = part_b[t].T

    @pl.when(pos == leaves - 1)
    def _():
        sep_out[...] = jnp.zeros_like(sep_out)

    gather_use(LAST_GATHER, gather_c, acc_l, lu_h, lu_l, False, None, False)
    solved_l[...] = solved_l[...] - acc_l[...]
    sum_scatter(
        LAST_SUM,
        solved_l,
        part_c,
        one_c,
        two_c,
        li_h,
        li_l,
        True,
        None,
        False,
        lambda p: None,
    )
    leaf_out[...] = part_c[t].T
    for outer, cond, wait in pending:
        when(outer, lambda cond=cond, wait=wait: when(cond, wait))


def body(rhs_leaf, rhs_sep, leaf_inv, leaf_up, sep_inv, sep_up, live_tiles):
    leaves = lax.axis_size("leaf")
    tall, cols = rhs_leaf.shape
    share = rhs_sep.shape[0]
    whole = 4 * share
    any_space = pl.BlockSpec(memory_space=pl.ANY)

    def f32(*shape):
        return pltpu.VMEM(shape, F32)

    weights = [(4, tall, tall), (4, share, tall), (4, share, share), (4, share, share)]
    halves = [pltpu.VMEM(shape, BF16) for shape in weights for _ in range(2)]
    scratch = (
        [f32(tall, cols), f32(share, cols)]
        + [f32(*shape) for shape in weights]
        + halves
        + [f32(4, cols, tall)]
        + [f32(4, cols, share)] * 3
        + [f32(4, cols, share)] * 3
        + [f32(4, cols, tall)]
        + [f32(2, cols, share)] * 3
        + [f32(2, cols, tall)]
        + [f32(cols, share)] * 3
        + [f32(cols, tall)]
        + [f32(2, cols, share), f32(cols, tall), f32(cols, share), f32(cols, share), f32(cols, tall)]
        + [
            pltpu.SemaphoreType.DMA((5, 4)),
            pltpu.SemaphoreType.DMA((KINDS + 1, PIECES)),
            pltpu.SemaphoreType.DMA((KINDS + 1, PIECES)),
        ]
    )
    work = 4 * cols * (tall * 4 * tall + whole * tall + 2 * whole * share)
    return tuple(
        pl.pallas_call(
            functools.partial(kernel, leaves),
            out_shape=(
                jax.ShapeDtypeStruct((tall, cols), F32),
                jax.ShapeDtypeStruct((share, cols), F32),
            ),
            in_specs=[pl.BlockSpec(memory_space=pltpu.SMEM)] + [any_space] * 6,
            out_specs=(
                pl.BlockSpec(memory_space=pltpu.VMEM),
                pl.BlockSpec(memory_space=pltpu.VMEM),
            ),
            scratch_shapes=scratch,
            compiler_params=pltpu.CompilerParams(
                collective_id=0, has_side_effects=True, vmem_limit_bytes=56 * 1024 * 1024
            ),
            cost_estimate=pl.CostEstimate(flops=work, bytes_accessed=12 << 20, transcendentals=0),
        )(live_tiles, rhs_leaf, rhs_sep, leaf_inv, leaf_up[0], sep_inv, sep_up[0])
    )


def solution(mesh):
    return jax.shard_map(
        body,
        mesh=mesh,
        in_specs=(
            P(("leaf", "tile"), None),
            P(("leaf", "tile"), None),
            P(("leaf", "tile"), None),
            P("leaf", None, "tile"),
            P(("leaf", "tile"), None),
            P("leaf", None, "tile"),
            P(),
        ),
        out_specs=(P(("leaf", "tile"), None), P(("leaf", "tile"), None)),
        check_vma=False,
    )
```

```python
import functools
import jax
import jax.numpy as jnp
from jax import lax
from jax.experimental import pallas as pl
from jax.experimental.pallas import tpu as pltpu
from jax.sharding import PartitionSpec as P

TILE = 128
PIECES = 2
SKEW = 1
MESH = pl.DeviceIdType.MESH
F32 = jnp.float32
BF16 = jnp.bfloat16

LEAF_GATHER, LEAF_SUM, SEP_GATHER, SEP_SUM = 0, 3, 6, 9
BACK_GATHER, BACK_SUM, LAST_GATHER, LAST_SUM = 12, 15, 18, 21
KID, ABOVE, LEAF_ABOVE, ABOVE_RIGHT = 24, 26, 27, 28
KINDS = 29


def split(value):
    high = value.astype(BF16)
    return high, (value - high.astype(F32)).astype(BF16)


def times(value, high_ref, low_ref, index, transposed):
    dims = (((1,), (1 if transposed else 0,)), ((), ()))
    rows = value.shape[0]
    high, low = split(value)
    both = jnp.concatenate([high, low], axis=0)
    first = lax.dot_general(both, high_ref[index], dims, preferred_element_type=F32)
    second = lax.dot_general(high, low_ref[index], dims, preferred_element_type=F32)
    return first[:rows] + first[rows:] + second


def kernel(
    leaves,
    live_ref,
    rhs_leaf,
    rhs_sep,
    leaf_inv,
    leaf_up,
    sep_inv,
    sep_up,
    leaf_out,
    sep_out,
    rhs_l,
    rhs_s,
    li,
    lu,
    si,
    su,
    li_h,
    li_l,
    lu_h,
    lu_l,
    si_h,
    si_l,
    su_h,
    su_l,
    gather_l,
    gather_s,
    gather_b,
    gather_c,
    part_l,
    part_s,
    part_b,
    part_c,
    one_l,
    one_s,
    one_b,
    one_c,
    two_l,
    two_s,
    two_b,
    two_c,
    kid,
    solved_l,
    solved_s,
    acc_s,
    acc_l,
    load_sem,
    send_sem,
    recv_sem,
):
    depth = leaves.bit_length() - 1
    first_block = leaves // 4 + 1
    leaf = lax.axis_index("leaf")
    t = lax.axis_index("tile")
    core = t % 2
    half = t // 2
    sib = t + 1 - 2 * core
    acr = (t + 2) % 4
    far = (sib + 2) % 4
    pos = (leaf + leaves - first_block) % leaves
    ahead = pos + 1
    share = rhs_s.shape[0]
    cols = rhs_s.shape[1]
    rows = cols // PIECES

    def block_of(place):
        return (place + leaves + first_block) % leaves

    level_one = ahead % 2 == 1
    has_sep = pos < leaves - 1
    is_top = ahead == leaves // 2
    not_top = jnp.logical_and(has_sep, ahead != leaves // 2)
    has_kids = jnp.logical_and(has_sep, ahead % 2 == 0)
    parent = pos * 0
    side = pos * 0
    reach = pos * 0
    for level in range(1, depth + 1):
        own = (ahead % (1 << level) == (1 << (level - 1))).astype(jnp.int32)
        odd = (ahead // (1 << level)) % 2
        step = 1 << (level - 1)
        parent = parent + own * (pos + step - 2 * step * odd)
        side = side + own * odd
        reach = reach + own * (step // 2)
    up_block = block_of(parent)
    left_block = block_of(pos - reach)
    right_block = block_of(pos + reach)
    pair_block = block_of(pos + 1 - 2 * (pos % 2))

    def loads(kind, source, target, by_column):
        out = []
        for q in range(4):
            if by_column:
                width = target.shape[2]
                view = source.at[:, pl.ds(q * width, width)]
            else:
                height = target.shape[1]
                view = source.at[pl.ds(q * height, height), :]
            out.append(pltpu.make_async_copy(view, target.at[q], load_sem.at[kind, q]))
        return out

    load_rl = pltpu.make_async_copy(rhs_leaf, rhs_l, load_sem.at[4, 0])
    load_rs = pltpu.make_async_copy(rhs_sep, rhs_s, load_sem.at[4, 1])
    load_li = loads(0, leaf_inv, li, True)
    load_lu = loads(1, leaf_up, lu, False)
    load_si = loads(2, sep_inv, si, True)
    load_su = loads(3, sep_up, su, False)
    load_rl.start()
    for copy in load_li + load_lu:
        copy.start()
    load_rs.start()
    for copy in load_si + load_su:
        copy.start()

    barrier = pltpu.get_barrier_semaphore()

    def greet(block, tile):
        pl.semaphore_signal(barrier, inc=1, device_id=(block, tile), device_id_type=MESH)

    greet(leaf, sib)
    greet(leaf, acr)
    greet(pair_block, t)

    @pl.when(not_top)
    def _():
        greet(up_block, t)

    @pl.when(has_kids)
    def _():
        greet(left_block, t)
        greet(right_block, t)

    def split_weights(copies, source, high, low):
        for q in range(4):
            copies[q].wait()
            height = source.shape[1]

            def body(i, carry, q=q):
                at = pl.ds(pl.multiple_of(i * 64, 64), 64)
                h, l = split(source[q, at, :])
                high[q, at, :] = h
                low[q, at, :] = l
                return carry

            lax.fori_loop(0, height // 64, body, 0)

    load_rl.wait()
    gather_l[t] = rhs_l[...].T

    pl.semaphore_wait(
        barrier, 3 + not_top.astype(jnp.int32) + 2 * has_kids.astype(jnp.int32)
    )

    pending = []

    def when(conds, run):
        conds = [cond for cond in conds if cond is not None]
        if not conds:
            run()
        else:
            pl.when(conds[0])(lambda: when(conds[1:], run))

    def at(p):
        return pl.ds(p * rows, rows)

    def piece(ref, q, p):
        return lambda: ref.at[at(p)] if q is None else ref.at[q, at(p)]

    def send(kind, p, source, target, block, tile, outer, gate, slot=None):
        def make():
            return pltpu.make_async_remote_copy(
                src_ref=source(),
                dst_ref=target(),
                send_sem=send_sem.at[kind, p],
                recv_sem=recv_sem.at[kind if slot is None else slot, p],
                device_id=(block, tile),
                device_id_type=MESH,
            )

        when(gate, lambda: make().start())
        pending.append((outer + gate, lambda: make().wait_send()))

    def arrive(kind, p, target):
        pltpu.make_async_remote_copy(
            src_ref=target(),
            dst_ref=target(),
            send_sem=send_sem.at[kind, p],
            recv_sem=recv_sem.at[kind, p],
            device_id=(leaf, sib),
            device_id_type=MESH,
        ).wait_recv()

    def run(chain):
        chains = [chain(p) for p in range(PIECES)]
        alive = [True] * PIECES
        turn = 0
        while any(alive):
            for p in range(PIECES):
                if alive[p] and turn >= SKEW * p:
                    alive[p] = next(chains[p], "end") != "end"
            turn += 1

    low_core, high_core = core == 0, core == 1
    low_half, high_half = half == 0, half == 1

    def gather_send(kind, ref, p, triangle, outer, gate):
        mine = piece(ref, t, p)
        send(kind + 1, p, mine, mine, leaf, acr, outer, gate + (low_half if triangle else None,))
        send(kind, p, mine, mine, leaf, sib, outer, gate + (low_core if triangle else None,))

    def gather_use(kind, ref, acc, high, low, triangle, outer, gate, transposed, p):
        cores = gate + (high_core if triangle else None,)
        halves = gate + (high_half if triangle else None,)

        def add(q):
            acc[at(p), :] += times(ref[q, at(p), :], high, low, q, transposed)

        def own():
            acc[at(p), :] = times(ref[t, at(p), :], high, low, t, transposed)

        def from_sib():
            arrive(kind, p, piece(ref, sib, p))
            add(sib)

        def from_far():
            arrive(kind + 2, p, piece(ref, far, p))
            add(far)

        when(gate, own)
        yield
        when(cores, from_sib)
        got = piece(ref, acr, p)
        when(halves, lambda: arrive(kind + 1, p, got))
        send(kind + 2, p, got, got, leaf, sib, outer, halves)
        when(halves, lambda: add(acr))
        yield
        when(halves, from_far)

    def sum_scatter(kind, value, part, one, two, high, low, triangle, outer, gate, transposed, p):
        over = gate + (high_half if triangle else None,)
        giving = gate + (high_core if triangle else None,)
        taking = gate + (low_core if triangle else None,)
        taking_far = gate + (low_half if triangle else None,)

        def work(q):
            part[q, at(p), :] = times(value[at(p), :], high, low, q, transposed)

        when(over, lambda: work(far))
        send(kind, p, piece(part, far, p), piece(one, 0, p), leaf, sib, outer, over)
        when(over, lambda: work(acr))
        when(giving, lambda: work(sib))
        send(kind + 2, p, piece(part, sib, p), piece(one, 1, p), leaf, sib, outer, giving)
        yield

        def pass_on():
            arrive(kind, p, piece(one, 0, p))
            part[acr, at(p), :] += one[0, at(p), :]

        when(over, pass_on)
        send(kind + 1, p, piece(part, acr, p), piece(two, None, p), leaf, acr, outer, over)
        when(gate, lambda: work(t))

        def from_sib():
            arrive(kind + 2, p, piece(one, 1, p))
            part[t, at(p), :] += one[1, at(p), :]

        when(taking, from_sib)
        yield

        def from_acr():
            arrive(kind + 1, p, piece(two, None, p))
            part[t, at(p), :] += two[at(p), :]

        when(taking_far, from_acr)

    is_odd = pos % 2 == 1
    is_even = pos % 2 == 0
    for p in range(PIECES):
        gather_send(LEAF_GATHER, gather_l, p, True, (), ())
    split_weights(load_li, li, li_h, li_l)
    split_weights(load_lu, lu, lu_h, lu_l)

    def leaf_up_chain(p):
        yield from gather_use(
            LEAF_GATHER, gather_l, solved_l, li_h, li_l, True, (), (), True, p
        )
        yield from sum_scatter(
            LEAF_SUM, solved_l, part_l, one_l, two_l, lu_h, lu_l, False, (), (), True, p
        )

        @pl.when(is_even)
        def _():
            kid[0, at(p), :] = part_l[t, at(p), :]

        send(
            KID, p, piece(part_l, t, p), piece(kid, 1, p), pair_block, t, (), (is_odd,), KID + 1
        )

    run(leaf_up_chain)
    split_weights(load_si, si, si_h, si_l)
    split_weights(load_su, su, su_h, su_l)
    load_rs.wait()

    live = live_ref[leaf]
    index = lax.broadcasted_iota(jnp.int32, (1, share), 1) + t * share
    mask = jnp.where(index < live * TILE, 1.0, 0.0).astype(F32)

    @pl.when(has_sep)
    def _():
        inside = (has_sep,)
        linked = (not_top,)
        acc_s[...] = rhs_s[...].T

        def sep_up_chain(p):
            when((has_kids,), lambda: arrive(KID, p, piece(kid, 0, p)))
            arrive(KID + 1, p, piece(kid, 1, p))
            gather_s[t, at(p), :] = (
                acc_s[at(p), :] - kid[0, at(p), :] - kid[1, at(p), :]
            ) * mask
            gather_send(SEP_GATHER, gather_s, p, True, inside, ())
            yield from gather_use(
                SEP_GATHER, gather_s, solved_s, si_h, si_l, True, inside, (), True, p
            )
            solved_s[at(p), :] = solved_s[at(p), :] * mask
            yield from sum_scatter(
                SEP_SUM, solved_s, part_s, one_s, two_s, su_h, su_l, False, inside, linked, True, p
            )

            def make():
                return pltpu.make_async_remote_copy(
                    src_ref=part_s.at[t, at(p)],
                    dst_ref=kid.at[side, at(p)],
                    send_sem=send_sem.at[ABOVE_RIGHT, p],
                    recv_sem=recv_sem.at[KID + side, p],
                    device_id=(up_block, t),
                    device_id_type=MESH,
                )

            when(linked, lambda: make().start())
            pending.append((inside + linked, lambda: make().wait_send()))

        run(sep_up_chain)

        def sep_down_chain(p):
            when(linked, lambda: arrive(ABOVE, p, piece(gather_b, t, p)))
            gather_send(BACK_GATHER, gather_b, p, False, inside, linked)
            yield from gather_use(
                BACK_GATHER, gather_b, acc_s, su_h, su_l, False, inside, linked, False, p
            )

            @pl.when(not_top)
            def _():
                solved_s[at(p), :] = (solved_s[at(p), :] - acc_s[at(p), :]) * mask

            yield from sum_scatter(
                BACK_SUM, solved_s, part_b, one_b, two_b, si_h, si_l, True, inside, (), False, p
            )
            part_b[t, at(p), :] = part_b[t, at(p), :] * mask
            mine = piece(part_b, t, p)
            there = piece(gather_b, t, p)
            here = piece(gather_c, t, p)
            send(ABOVE, p, mine, there, left_block, t, inside, (has_kids,))
            send(ABOVE_RIGHT + 1, p, mine, there, right_block, t, inside, (has_kids,), ABOVE)
            send(LEAF_ABOVE, p, mine, here, pair_block, t, inside, (level_one,))

            @pl.when(level_one)
            def _():
                gather_c[t, at(p), :] = part_b[t, at(p), :]

        run(sep_down_chain)
        sep_out[...] = part_b[t].T

    @pl.when(pos == leaves - 1)
    def _():
        sep_out[...] = jnp.zeros_like(sep_out)

    def leaf_down_chain(p):
        when((is_odd,), lambda: arrive(LEAF_ABOVE, p, piece(gather_c, t, p)))
        gather_send(LAST_GATHER, gather_c, p, False, (), ())
        yield from gather_use(
            LAST_GATHER, gather_c, acc_l, lu_h, lu_l, False, (), (), False, p
        )
        solved_l[at(p), :] = solved_l[at(p), :] - acc_l[at(p), :]
        yield from sum_scatter(
            LAST_SUM, solved_l, part_c, one_c, two_c, li_h, li_l, True, (), (), False, p
        )

    run(leaf_down_chain)
    leaf_out[...] = part_c[t].T
    for conds, wait in pending:
        when(conds, wait)


def body(rhs_leaf, rhs_sep, leaf_inv, leaf_up, sep_inv, sep_up, live_tiles):
    leaves = lax.axis_size("leaf")
    tall, cols = rhs_leaf.shape
    share = rhs_sep.shape[0]
    whole = 4 * share
    any_space = pl.BlockSpec(memory_space=pl.ANY)

    def f32(*shape):
        return pltpu.VMEM(shape, F32)

    weights = [(4, tall, tall), (4, share, tall), (4, share, share), (4, share, share)]
    halves = [pltpu.VMEM(shape, BF16) for shape in weights for _ in range(2)]
    scratch = (
        [f32(tall, cols), f32(share, cols)]
        + [f32(*shape) for shape in weights]
        + halves
        + [f32(4, cols, tall)]
        + [f32(4, cols, share)] * 3
        + [f32(4, cols, share)] * 3
        + [f32(4, cols, tall)]
        + [f32(2, cols, share)] * 3
        + [f32(2, cols, tall)]
        + [f32(cols, share)] * 3
        + [f32(cols, tall)]
        + [f32(2, cols, share), f32(cols, tall), f32(cols, share), f32(cols, share), f32(cols, tall)]
        + [
            pltpu.SemaphoreType.DMA((5, 4)),
            pltpu.SemaphoreType.DMA((KINDS + 1, PIECES)),
            pltpu.SemaphoreType.DMA((KINDS + 1, PIECES)),
        ]
    )
    work = 4 * cols * (tall * 4 * tall + whole * tall + 2 * whole * share)
    return tuple(
        pl.pallas_call(
            functools.partial(kernel, leaves),
            out_shape=(
                jax.ShapeDtypeStruct((tall, cols), F32),
                jax.ShapeDtypeStruct((share, cols), F32),
            ),
            in_specs=[pl.BlockSpec(memory_space=pltpu.SMEM)] + [any_space] * 6,
            out_specs=(
                pl.BlockSpec(memory_space=pltpu.VMEM),
                pl.BlockSpec(memory_space=pltpu.VMEM),
            ),
            scratch_shapes=scratch,
            compiler_params=pltpu.CompilerParams(
                collective_id=0, has_side_effects=True, vmem_limit_bytes=56 * 1024 * 1024
            ),
            cost_estimate=pl.CostEstimate(flops=work, bytes_accessed=12 << 20, transcendentals=0),
        )(live_tiles, rhs_leaf, rhs_sep, leaf_inv, leaf_up[0], sep_inv, sep_up[0])
    )


def solution(mesh):
    return jax.shard_map(
        body,
        mesh=mesh,
        in_specs=(
            P(("leaf", "tile"), None),
            P(("leaf", "tile"), None),
            P(("leaf", "tile"), None),
            P("leaf", None, "tile"),
            P(("leaf", "tile"), None),
            P("leaf", None, "tile"),
            P(),
        ),
        out_specs=(P(("leaf", "tile"), None), P(("leaf", "tile"), None)),
        check_vma=False,
    )
```

```python
import functools
import jax
import jax.numpy as jnp
from jax import lax
from jax.experimental import pallas as pl
from jax.experimental.pallas import tpu as pltpu
from jax.sharding import PartitionSpec as P

TILE = 128
PIECES = 2
SKEW = 2
MESH = pl.DeviceIdType.MESH
F32 = jnp.float32
BF16 = jnp.bfloat16

LEAF_GATHER, LEAF_SUM, SEP_GATHER, SEP_SUM = 0, 3, 6, 9
BACK_GATHER, BACK_SUM, LAST_GATHER, LAST_SUM = 12, 15, 18, 21
KID, ABOVE, LEAF_ABOVE, ABOVE_RIGHT = 24, 26, 27, 28
KINDS = 29


def split(value):
    high = value.astype(BF16)
    return high, (value - high.astype(F32)).astype(BF16)


def times(value, high_ref, low_ref, index, transposed):
    dims = (((1,), (1 if transposed else 0,)), ((), ()))
    rows = value.shape[0]
    high, low = split(value)
    both = jnp.concatenate([high, low], axis=0)
    first = lax.dot_general(both, high_ref[index], dims, preferred_element_type=F32)
    second = lax.dot_general(high, low_ref[index], dims, preferred_element_type=F32)
    return first[:rows] + first[rows:] + second


def kernel(
    leaves,
    live_ref,
    rhs_leaf,
    rhs_sep,
    leaf_inv,
    leaf_up,
    sep_inv,
    sep_up,
    leaf_out,
    sep_out,
    rhs_l,
    rhs_s,
    li,
    lu,
    si,
    su,
    li_h,
    li_l,
    lu_h,
    lu_l,
    si_h,
    si_l,
    su_h,
    su_l,
    gather_l,
    gather_s,
    gather_b,
    gather_c,
    part_l,
    part_s,
    part_b,
    part_c,
    one_l,
    one_s,
    one_b,
    one_c,
    two_l,
    two_s,
    two_b,
    two_c,
    kid,
    solved_l,
    solved_s,
    acc_s,
    acc_l,
    load_sem,
    send_sem,
    recv_sem,
):
    depth = leaves.bit_length() - 1
    first_block = leaves // 4 + 1
    leaf = lax.axis_index("leaf")
    t = lax.axis_index("tile")
    core = t % 2
    half = t // 2
    sib = t + 1 - 2 * core
    acr = (t + 2) % 4
    far = (sib + 2) % 4
    pos = (leaf + leaves - first_block) % leaves
    ahead = pos + 1
    share = rhs_s.shape[0]
    cols = rhs_s.shape[1]
    rows = cols // PIECES

    def block_of(place):
        return (place + leaves + first_block) % leaves

    level_one = ahead % 2 == 1
    has_sep = pos < leaves - 1
    is_top = ahead == leaves // 2
    not_top = jnp.logical_and(has_sep, ahead != leaves // 2)
    has_kids = jnp.logical_and(has_sep, ahead % 2 == 0)
    parent = pos * 0
    side = pos * 0
    reach = pos * 0
    for level in range(1, depth + 1):
        own = (ahead % (1 << level) == (1 << (level - 1))).astype(jnp.int32)
        odd = (ahead // (1 << level)) % 2
        step = 1 << (level - 1)
        parent = parent + own * (pos + step - 2 * step * odd)
        side = side + own * odd
        reach = reach + own * (step // 2)
    up_block = block_of(parent)
    left_block = block_of(pos - reach)
    right_block = block_of(pos + reach)
    pair_block = block_of(pos + 1 - 2 * (pos % 2))

    def loads(kind, source, target, by_column):
        out = []
        for q in range(4):
            if by_column:
                width = target.shape[2]
                view = source.at[:, pl.ds(q * width, width)]
            else:
                height = target.shape[1]
                view = source.at[pl.ds(q * height, height), :]
            out.append(pltpu.make_async_copy(view, target.at[q], load_sem.at[kind, q]))
        return out

    load_rl = pltpu.make_async_copy(rhs_leaf, rhs_l, load_sem.at[4, 0])
    load_rs = pltpu.make_async_copy(rhs_sep, rhs_s, load_sem.at[4, 1])
    load_li = loads(0, leaf_inv, li, True)
    load_lu = loads(1, leaf_up, lu, False)
    load_si = loads(2, sep_inv, si, True)
    load_su = loads(3, sep_up, su, False)
    load_rl.start()
    for copy in load_li + load_lu:
        copy.start()
    load_rs.start()
    for copy in load_si + load_su:
        copy.start()

    barrier = pltpu.get_barrier_semaphore()

    def greet(block, tile):
        pl.semaphore_signal(barrier, inc=1, device_id=(block, tile), device_id_type=MESH)

    greet(leaf, sib)
    greet(leaf, acr)
    greet(pair_block, t)

    @pl.when(not_top)
    def _():
        greet(up_block, t)

    @pl.when(has_kids)
    def _():
        greet(left_block, t)
        greet(right_block, t)

    def split_weights(copies, source, high, low):
        for q in range(4):
            copies[q].wait()
            height = source.shape[1]

            def body(i, carry, q=q):
                at = pl.ds(pl.multiple_of(i * 64, 64), 64)
                h, l = split(source[q, at, :])
                high[q, at, :] = h
                low[q, at, :] = l
                return carry

            lax.fori_loop(0, height // 64, body, 0)

    load_rl.wait()
    gather_l[t] = rhs_l[...].T

    pl.semaphore_wait(
        barrier, 3 + not_top.astype(jnp.int32) + 2 * has_kids.astype(jnp.int32)
    )

    pending = []

    def when(conds, run):
        conds = [cond for cond in conds if cond is not None]
        if not conds:
            run()
        else:
            pl.when(conds[0])(lambda: when(conds[1:], run))

    def at(p):
        return pl.ds(p * rows, rows)

    def piece(ref, q, p):
        return lambda: ref.at[at(p)] if q is None else ref.at[q, at(p)]

    def send(kind, p, source, target, block, tile, outer, gate, slot=None):
        def make():
            return pltpu.make_async_remote_copy(
                src_ref=source(),
                dst_ref=target(),
                send_sem=send_sem.at[kind, p],
                recv_sem=recv_sem.at[kind if slot is None else slot, p],
                device_id=(block, tile),
                device_id_type=MESH,
            )

        when(gate, lambda: make().start())
        pending.append((outer + gate, lambda: make().wait_send()))

    def arrive(kind, p, target):
        pltpu.make_async_remote_copy(
            src_ref=target(),
            dst_ref=target(),
            send_sem=send_sem.at[kind, p],
            recv_sem=recv_sem.at[kind, p],
            device_id=(leaf, sib),
            device_id_type=MESH,
        ).wait_recv()

    def run(chain):
        chains = [chain(p) for p in range(PIECES)]
        alive = [True] * PIECES
        turn = 0
        while any(alive):
            for p in range(PIECES):
                if alive[p] and turn >= SKEW * p:
                    alive[p] = next(chains[p], "end") != "end"
            turn += 1

    low_core, high_core = core == 0, core == 1
    low_half, high_half = half == 0, half == 1

    def gather_send(kind, ref, p, triangle, outer, gate):
        mine = piece(ref, t, p)
        send(kind + 1, p, mine, mine, leaf, acr, outer, gate + (low_half if triangle else None,))
        send(kind, p, mine, mine, leaf, sib, outer, gate + (low_core if triangle else None,))

    def gather_use(kind, ref, acc, high, low, triangle, outer, gate, transposed, p):
        cores = gate + (high_core if triangle else None,)
        halves = gate + (high_half if triangle else None,)

        def add(q):
            acc[at(p), :] += times(ref[q, at(p), :], high, low, q, transposed)

        def own():
            acc[at(p), :] = times(ref[t, at(p), :], high, low, t, transposed)

        def from_sib():
            arrive(kind, p, piece(ref, sib, p))
            add(sib)

        def from_far():
            arrive(kind + 2, p, piece(ref, far, p))
            add(far)

        when(gate, own)
        yield
        when(cores, from_sib)
        got = piece(ref, acr, p)
        when(halves, lambda: arrive(kind + 1, p, got))
        send(kind + 2, p, got, got, leaf, sib, outer, halves)
        when(halves, lambda: add(acr))
        yield
        when(halves, from_far)

    def sum_scatter(kind, value, part, one, two, high, low, triangle, outer, gate, transposed, p):
        over = gate + (high_half if triangle else None,)
        giving = gate + (high_core if triangle else None,)
        taking = gate + (low_core if triangle else None,)
        taking_far = gate + (low_half if triangle else None,)

        def work(q):
            part[q, at(p), :] = times(value[at(p), :], high, low, q, transposed)

        when(over, lambda: work(far))
        send(kind, p, piece(part, far, p), piece(one, 0, p), leaf, sib, outer, over)
        when(over, lambda: work(acr))
        when(giving, lambda: work(sib))
        send(kind + 2, p, piece(part, sib, p), piece(one, 1, p), leaf, sib, outer, giving)
        yield

        def pass_on():
            arrive(kind, p, piece(one, 0, p))
            part[acr, at(p), :] += one[0, at(p), :]

        when(over, pass_on)
        send(kind + 1, p, piece(part, acr, p), piece(two, None, p), leaf, acr, outer, over)
        when(gate, lambda: work(t))

        def from_sib():
            arrive(kind + 2, p, piece(one, 1, p))
            part[t, at(p), :] += one[1, at(p), :]

        when(taking, from_sib)
        yield

        def from_acr():
            arrive(kind + 1, p, piece(two, None, p))
            part[t, at(p), :] += two[at(p), :]

        when(taking_far, from_acr)

    is_odd = pos % 2 == 1
    is_even = pos % 2 == 0
    for p in range(PIECES):
        gather_send(LEAF_GATHER, gather_l, p, True, (), ())
    split_weights(load_li, li, li_h, li_l)
    split_weights(load_lu, lu, lu_h, lu_l)

    def leaf_up_chain(p):
        yield from gather_use(
            LEAF_GATHER, gather_l, solved_l, li_h, li_l, True, (), (), True, p
        )
        sums = sum_scatter(
            LEAF_SUM, solved_l, part_l, one_l, two_l, lu_h, lu_l, False, (), (), True, p
        )
        next(sums)
        yield
        next(sums)
        if p == PIECES - 1:
            split_weights(load_si, si, si_h, si_l)
            split_weights(load_su, su, su_h, su_l)
            load_rs.wait()
        yield
        next(sums, None)

        @pl.when(is_even)
        def _():
            kid[0, at(p), :] = part_l[t, at(p), :]

        send(
            KID, p, piece(part_l, t, p), piece(kid, 1, p), pair_block, t, (), (is_odd,), KID + 1
        )

    run(leaf_up_chain)

    live = live_ref[leaf]
    index = lax.broadcasted_iota(jnp.int32, (1, share), 1) + t * share
    mask = jnp.where(index < live * TILE, 1.0, 0.0).astype(F32)

    @pl.when(has_sep)
    def _():
        inside = (has_sep,)
        linked = (not_top,)
        acc_s[...] = rhs_s[...].T

        def sep_up_chain(p):
            when((has_kids,), lambda: arrive(KID, p, piece(kid, 0, p)))
            arrive(KID + 1, p, piece(kid, 1, p))
            gather_s[t, at(p), :] = (
                acc_s[at(p), :] - kid[0, at(p), :] - kid[1, at(p), :]
            ) * mask
            gather_send(SEP_GATHER, gather_s, p, True, inside, ())
            yield from gather_use(
                SEP_GATHER, gather_s, solved_s, si_h, si_l, True, inside, (), True, p
            )
            solved_s[at(p), :] = solved_s[at(p), :] * mask
            yield from sum_scatter(
                SEP_SUM, solved_s, part_s, one_s, two_s, su_h, su_l, False, inside, linked, True, p
            )

            def make():
                return pltpu.make_async_remote_copy(
                    src_ref=part_s.at[t, at(p)],
                    dst_ref=kid.at[side, at(p)],
                    send_sem=send_sem.at[ABOVE_RIGHT, p],
                    recv_sem=recv_sem.at[KID + side, p],
                    device_id=(up_block, t),
                    device_id_type=MESH,
                )

            when(linked, lambda: make().start())
            pending.append((inside + linked, lambda: make().wait_send()))

        run(sep_up_chain)

        def sep_down_chain(p):
            when(linked, lambda: arrive(ABOVE, p, piece(gather_b, t, p)))
            gather_send(BACK_GATHER, gather_b, p, False, inside, linked)
            yield from gather_use(
                BACK_GATHER, gather_b, acc_s, su_h, su_l, False, inside, linked, False, p
            )

            @pl.when(not_top)
            def _():
                solved_s[at(p), :] = (solved_s[at(p), :] - acc_s[at(p), :]) * mask

            yield from sum_scatter(
                BACK_SUM, solved_s, part_b, one_b, two_b, si_h, si_l, True, inside, (), False, p
            )
            part_b[t, at(p), :] = part_b[t, at(p), :] * mask
            mine = piece(part_b, t, p)
            there = piece(gather_b, t, p)
            here = piece(gather_c, t, p)
            send(ABOVE, p, mine, there, left_block, t, inside, (has_kids,))
            send(ABOVE_RIGHT + 1, p, mine, there, right_block, t, inside, (has_kids,), ABOVE)
            send(LEAF_ABOVE, p, mine, here, pair_block, t, inside, (level_one,))

            @pl.when(level_one)
            def _():
                gather_c[t, at(p), :] = part_b[t, at(p), :]

        run(sep_down_chain)
        sep_out[...] = part_b[t].T

    @pl.when(pos == leaves - 1)
    def _():
        sep_out[...] = jnp.zeros_like(sep_out)

    def leaf_down_chain(p):
        when((is_odd,), lambda: arrive(LEAF_ABOVE, p, piece(gather_c, t, p)))
        gather_send(LAST_GATHER, gather_c, p, False, (), ())
        yield from gather_use(
            LAST_GATHER, gather_c, acc_l, lu_h, lu_l, False, (), (), False, p
        )
        solved_l[at(p), :] = solved_l[at(p), :] - acc_l[at(p), :]
        yield from sum_scatter(
            LAST_SUM, solved_l, part_c, one_c, two_c, li_h, li_l, True, (), (), False, p
        )

    run(leaf_down_chain)
    leaf_out[...] = part_c[t].T
    for conds, wait in pending:
        when(conds, wait)


def body(rhs_leaf, rhs_sep, leaf_inv, leaf_up, sep_inv, sep_up, live_tiles):
    leaves = lax.axis_size("leaf")
    tall, cols = rhs_leaf.shape
    share = rhs_sep.shape[0]
    whole = 4 * share
    any_space = pl.BlockSpec(memory_space=pl.ANY)

    def f32(*shape):
        return pltpu.VMEM(shape, F32)

    weights = [(4, tall, tall), (4, share, tall), (4, share, share), (4, share, share)]
    halves = [pltpu.VMEM(shape, BF16) for shape in weights for _ in range(2)]
    scratch = (
        [f32(tall, cols), f32(share, cols)]
        + [f32(*shape) for shape in weights]
        + halves
        + [f32(4, cols, tall)]
        + [f32(4, cols, share)] * 3
        + [f32(4, cols, share)] * 3
        + [f32(4, cols, tall)]
        + [f32(2, cols, share)] * 3
        + [f32(2, cols, tall)]
        + [f32(cols, share)] * 3
        + [f32(cols, tall)]
        + [f32(2, cols, share), f32(cols, tall), f32(cols, share), f32(cols, share), f32(cols, tall)]
        + [
            pltpu.SemaphoreType.DMA((5, 4)),
            pltpu.SemaphoreType.DMA((KINDS + 1, PIECES)),
            pltpu.SemaphoreType.DMA((KINDS + 1, PIECES)),
        ]
    )
    work = 4 * cols * (tall * 4 * tall + whole * tall + 2 * whole * share)
    return tuple(
        pl.pallas_call(
            functools.partial(kernel, leaves),
            out_shape=(
                jax.ShapeDtypeStruct((tall, cols), F32),
                jax.ShapeDtypeStruct((share, cols), F32),
            ),
            in_specs=[pl.BlockSpec(memory_space=pltpu.SMEM)] + [any_space] * 6,
            out_specs=(
                pl.BlockSpec(memory_space=pltpu.VMEM),
                pl.BlockSpec(memory_space=pltpu.VMEM),
            ),
            scratch_shapes=scratch,
            compiler_params=pltpu.CompilerParams(
                collective_id=0, has_side_effects=True, vmem_limit_bytes=56 * 1024 * 1024
            ),
            cost_estimate=pl.CostEstimate(flops=work, bytes_accessed=12 << 20, transcendentals=0),
        )(live_tiles, rhs_leaf, rhs_sep, leaf_inv, leaf_up[0], sep_inv, sep_up[0])
    )


def solution(mesh):
    return jax.shard_map(
        body,
        mesh=mesh,
        in_specs=(
            P(("leaf", "tile"), None),
            P(("leaf", "tile"), None),
            P(("leaf", "tile"), None),
            P("leaf", None, "tile"),
            P(("leaf", "tile"), None),
            P("leaf", None, "tile"),
            P(),
        ),
        out_specs=(P(("leaf", "tile"), None), P(("leaf", "tile"), None)),
        check_vma=False,
    )
```
